256 devices in a mesh: rows: 16 (over z, x_hi), vocab: 16 (over x_lo, y, core).
Axes of the slice: x: 4 (x_hi: 2, x_lo: 2; x = x_hi * 2 + x_lo), y: 4, z: 8, core: 2. Of those that a mesh axis runs over, the one named last changes fastest.
Arguments:
- hidden_rows: bfloat16 [512, 8192], P('vocab', 'rows'), may hold values from -24 to 24
- row_states: int32 [512], P('vocab'), may hold values from 0 to 511
- head_weight: bfloat16 [8192, 152064], P(None, ('rows', 'vocab')), may hold values from -2 to 2
- grammar_table: int32 [512, 152064], P(None, ('rows', 'vocab')), may hold values from 0 to 1, as said below
Outputs:
- log_probs: float32 [512, 152064], P(None, ('rows', 'vocab'))
- normalizer: float32 [512], replicated
The draws below stay inside these ranges and needn't reach their ends.
Inputs may be any that keep to these rules, and one draw needn't show every extreme that they name: `grammar_table`: every state allows the tokens 0 to 31.
All inputs are finite; a program needn't handle non-finite values.
Results may differ from the reference program's by a relative error of at most 0.0003.
Values may be sent and summed in bfloat16 or wider, within the bound.
A program may use at most 64 MiB of HBM per device.

```python
import math
import jax
import jax.numpy as jnp

D = 8192
VOCAB = 152064
STATES = 512
ROWS = 512


def draw_hidden_rows(key, part):
    key_scale = jax.random.fold_in(key, 11)
    key_values = jax.random.fold_in(key, 13)
    scales = jnp.exp(jax.random.uniform(key_scale, (ROWS, 1), minval=math.log(0.5), maxval=math.log(5.0)))
    entries = jnp.clip(jax.random.normal(key_values, (ROWS, D)), -4.0, 4.0) * scales
    return entries.astype(jnp.bfloat16)


def draw_head_weight(key, part):
    key_scale = jax.random.fold_in(key, 21)
    key_values = jax.random.fold_in(key, 22)
    col_scale = jnp.exp(jax.random.uniform(key_scale, (1, VOCAB), minval=math.log(0.4), maxval=math.log(4.0)))
    sample = jnp.clip(jax.random.normal(key_values, (D, VOCAB)), -4.0, 4.0)
    general = sample * col_scale / math.sqrt(D)
    block_rows = D // 32
    weight = 2.0 / math.sqrt(block_rows)
    special = jnp.where(jnp.arange(D)[:, None] // block_rows == jnp.arange(32)[None, :], weight, 0.0)
    return jnp.concatenate([special, general[:, 32:]], axis=1).astype(jnp.bfloat16)


def draw_grammar_table(key, part):
    key_rate = jax.random.fold_in(key, 31)
    key_tiles = jax.random.fold_in(key, 32)
    key_ticket = jax.random.fold_in(key, 33)
    tile_count = (VOCAB + 127) // 128
    thresh = jax.random.randint(key_rate, (STATES, 1), 16, 600)
    tile_flags = jax.random.randint(key_tiles, (STATES, tile_count), 0, 3) > 0
    tile_on = jnp.repeat(tile_flags, 128, axis=1)[:, :VOCAB]
    ticket = jax.random.randint(key_ticket, (STATES, VOCAB), 0, 1024)
    allowed = (ticket < thresh) & tile_on
    allowed = allowed | (jnp.arange(VOCAB)[None, :] < 32)
    return allowed.astype(jnp.int32)


def touch_ends(drawn, own_key, smallest, top_value):
    longest = drawn.shape.index(max(drawn.shape))
    spots = []
    for shift in (0, 1):
        where = [jax.random.randint(jax.random.fold_in(own_key, axis), (), 0, length) for axis, length in enumerate(drawn.shape)]
        where[longest] = (where[longest] + shift) % drawn.shape[longest]
        spots.append(tuple(where))
    return drawn.at[spots[0]].set(smallest).at[spots[1]].set(top_value)


def setup_inputs(seed: int = 0) -> dict:
    key_of = jax.random.split(jax.random.key(seed), 5)
    hidden_rows = draw_hidden_rows(jax.random.fold_in(key_of[4], 71), 0)
    row_states = touch_ends(jax.random.randint(key_of[1], (ROWS,), 0, STATES), jax.random.fold_in(key_of[1], 1), 0, STATES - 1).astype(jnp.int32)
    head_weight = draw_head_weight(jax.random.fold_in(key_of[4], 71), 0)
    grammar_table = draw_grammar_table(jax.random.fold_in(key_of[4], 71), 0)
    return {"hidden_rows": hidden_rows, "row_states": row_states, "head_weight": head_weight, "grammar_table": grammar_table}


lowest = -1.0e30


def reference(hidden_rows, row_states, head_weight, grammar_table):
    logits = jnp.dot(hidden_rows, head_weight, preferred_element_type=jnp.float32)
    allowed = jnp.take(grammar_table, row_states.astype(jnp.int32), axis=0) > 0
    masked = jnp.where(allowed, logits, lowest)
    row_peak = jnp.max(masked, axis=1)
    exp_total = jnp.sum(jnp.where(allowed, jnp.exp(logits - row_peak[:, None]), 0.0), axis=1)
    normalizer = row_peak + jnp.log(exp_total)
    log_probs = jnp.where(allowed, logits - normalizer[:, None], 0.0)
    return log_probs, normalizer
```

```python
import jax
import jax.numpy as jnp
from jax import lax
from jax.sharding import PartitionSpec as P

lowest = -1e30


def local(hidden_rows, row_states, head_weight, grammar_table):
    state_count = grammar_table.shape[0]
    block = lax.all_gather(hidden_rows, "vocab", axis=0, tiled=True)
    states = lax.all_gather(row_states, "vocab", axis=0, tiled=True)
    every = lax.all_gather(block, "rows", axis=1, tiled=True)
    onehot = (jnp.arange(state_count, dtype=jnp.int32)[:, None] == states[None, :]).astype(jnp.bfloat16)
    allowed = (
        lax.dot_general(
            grammar_table.astype(jnp.bfloat16),
            onehot,
            (((0,), (0,)), ((), ())),
            preferred_element_type=jnp.float32,
        )
        > 0.5
    )
    logits = lax.dot_general(
        head_weight, every, (((0,), (1,)), ((), ())), preferred_element_type=jnp.float32
    )
    masked = jnp.where(allowed, logits, lowest)
    own_peak = jnp.max(masked, axis=0)
    own_total = jnp.sum(jnp.where(allowed, jnp.exp(masked - own_peak[None, :]), 0.0), axis=0)
    row_peak = lax.pmax(own_peak, ("rows", "vocab"))
    exp_total = lax.psum(own_total * jnp.exp(own_peak - row_peak), ("rows", "vocab"))
    normalizer = row_peak + jnp.log(exp_total)
    log_probs = jnp.where(allowed, logits - normalizer[None, :], 0.0)
    return (log_probs.T, normalizer)


def solution(mesh):
    placed = (
        P("vocab", "rows"),
        P("vocab"),
        P(None, ("rows", "vocab")),
        P(None, ("rows", "vocab")),
    )
    return jax.shard_map(
        local,
        mesh=mesh,
        in_specs=placed,
        out_specs=(P(None, ("rows", "vocab")), P()),
        check_vma=False,
    )
```

```python
import functools
import heapq
import itertools

import jax
import jax.numpy as jnp
from jax import lax
from jax.experimental import pallas as pl
from jax.experimental.pallas import tpu as pltpu
from jax.sharding import PartitionSpec as P

LOWEST = -1e30
NX, NY, NZ = 4, 4, 8
MESH = pl.DeviceIdType.MESH
HOP = 1.0
RATE = 46e3
NT = (((1,), (1,)), ((), ()))


def place(x, y, z, c):
    rows = z * 2 + lax.div(x, 2)
    vocab = lax.rem(x, 2) * 8 + y * 2 + c
    return (rows, vocab)


def b_first(z):
    return lax.div(z, 4) * 6 + lax.rem(z, 4)


def b_second(z):
    even = lax.div(z, 4) * 6 + 4 + lax.div(lax.rem(z, 4), 2)
    return jnp.where(lax.rem(z, 2) == 0, even, 12 + lax.div(z, 2))


def c_second(z):
    return jnp.where(lax.rem(z, 2) == 1, 8, 12) + lax.div(z, 2)


def kernel(
    hid, st_in, w_in, tab_in, acc_out, norm_out,
    ha, hb, hc, st, w, tab, ls, send, recv, near_send, near_recv, local,
):
    r, v = lax.axis_index("rows"), lax.axis_index("vocab")
    z, x = lax.div(r, 2), lax.rem(r, 2) * 2 + lax.div(v, 8)
    y, c = lax.rem(lax.div(v, 2), NY), lax.rem(v, 2)
    other = 1 - c
    columns = w_in.shape[0]

    def along(axis, step):
        size = {"x": NX, "y": NY, "z": NZ}[axis]
        at = {"x": x, "y": y, "z": z}
        at[axis] = lax.rem(at[axis] + size + step, size)
        return place(at["x"], at["y"], at["z"], c)

    partner = place(x, y, z, other)
    x_lo = lax.rem(x, 2)
    x_flip = place(x + 1 - 2 * x_lo, y, z, c)

    fills = []

    def fill(source, target):
        copy = pltpu.make_async_copy(source, target, local.at[len(fills)])
        copy.start()
        fills.append(copy)
        return copy

    quarter = [hid.at[:, pl.ds(128 * q, 128)] for q in range(4)]
    fill(quarter[0], ha.at[c, z, y, x])
    fill(quarter[1], hb.at[c, x, b_first(z), y])
    fill(quarter[2], hb.at[c, x, b_second(z), y])
    fill(quarter[3], hc.at[c, y, x, z])
    fill(quarter[2], hc.at[c, y, x, c_second(z)])
    fill(st_in, st.at[c, y, x_lo])
    tab_fill = fill(tab_in, tab)
    w_fill = fill(w_in, w)

    barrier = pltpu.get_barrier_semaphore()
    friends = [along(a, s) for a in "xyz" for s in (1, -1)] + [partner]
    for friend in friends:
        pl.semaphore_signal(barrier, inc=1, device_id=friend, device_id_type=MESH)
    pl.semaphore_wait(barrier, len(friends))
    for copy in fills[:6]:
        copy.wait()

    count = itertools.count()
    near_count = itertools.count()
    sent = []

    def remote(source, device, index, sends, recvs):
        copy = pltpu.make_async_remote_copy(
            src_ref=source, dst_ref=source, send_sem=sends.at[index],
            recv_sem=recvs.at[index], device_id=device, device_id_type=MESH,
        )
        copy.start()
        sent.append(copy)

    def arrived(target, index, recvs):
        pltpu.make_async_copy(target, target, recvs.at[index]).wait()

    def ring(axis, size, pos, piece, nbytes, start, seen):
        half = size // 2
        index = {}
        for d in range(1, half + 1):
            for way in (1, -1):
                for h in (0, 1):
                    if d < half or h == (0 if way > 0 else 1):
                        index[way, d, h] = next(count)
        step = nbytes / RATE
        when = {}
        for way in (1, -1):
            order = (0, 1) if way > 0 else (1, 0)
            for h in order:
                remote(piece(pos, h), along(axis, way), index[way, 1, h], send, recv)
            free = start
            for d in range(1, half + 1):
                for h in order:
                    if (way, d, h) in index:
                        ready = start if d == 1 else when[way, d - 1, h]
                        free = max(free, ready) + step
                        when[way, d, h] = free + HOP
        for key in sorted(index, key=lambda k: (when[k], k[1], -k[0])):
            way, d, h = key
            yield when[key]
            origin = lax.rem(pos + size - way * d, size)
            arrived(piece(origin, h), index[key], recv)
            if (way, d + 1, h) in index:
                remote(piece(origin, h), along(axis, way), index[way, d + 1, h], send, recv)
            seen(way, d, h, origin, when[key])
        return max(when.values())

    def ignore(*_):
        return None

    queue = []
    order = itertools.count()

    def push(time, action):
        heapq.heappush(queue, (time, next(order), action))

    def drive(generator):
        def action():
            try:
                time = next(generator)
            except StopIteration:
                return
            push(time, action)

        action()

    waits = {}

    def hand_over(name, piece, pos, h, time, key, nbytes):
        index = next(near_count)
        remote(piece(c, pos, h), partner, index, near_send, near_recv)
        waits[name, key, h] = (piece(other, pos, h), index, time + 1.0 + nbytes / 2e5)
        return waits[name, key, h][2]

    def gather(name, phases, piece, nbytes, done):
        start = 0.0
        for number, (axis, size, pos, part, part_bytes) in enumerate(phases):
            last = number == len(phases) - 1
            if last:
                for h in (0, 1):
                    ready = hand_over(name, piece, pos, h, start, (0, 0), nbytes)
                    done((0, 0), h, pos, ready)

                def seen(way, d, h, origin, time):
                    key = (way, d) if d < size // 2 else (0, d)
                    ready = hand_over(name, piece, origin, h, time, key, nbytes)
                    done(key, h, origin, ready)
            else:
                seen = ignore
            start = yield from ring(axis, size, pos, part, part_bytes, start, seen)

    def received(name, key, h):
        target, index, _ = waits[name, key, h]
        arrived(target, index, near_recv)

    block = 32 * 128 * 2
    a_piece = lambda core, p, h: ha.at[core, p, pl.ds(2 * h, 2)]
    b_piece = lambda core, p, h: hb.at[core, p, pl.ds(6 * h, 6)]
    c_piece = lambda core, p, h: hc.at[core, p, pl.ds(2 * h, 2), pl.ds(0, 12)]

    def weights(offsets):
        return jnp.concatenate(
            [w[:, pl.ds(pl.multiple_of(o, 128), 128)] for o in offsets], axis=1
        )

    def stack(parts):
        return jnp.concatenate(parts, axis=0)

    def a_task(zz):
        rhs = jnp.concatenate(
            [
                stack(
                    [
                        ha[core, zz, yy, 2 * hi + lo]
                        for lo in range(2) for yy in range(NY) for core in range(2)
                    ]
                )
                for hi in range(2)
            ],
            axis=1,
        )
        lhs = weights([(2 * zz + hi) * 512 for hi in range(2)])
        acc_out[...] += lax.dot_general(lhs, rhs, NT, preferred_element_type=jnp.float32)

    def b_task(xx, h):
        hi, lo = lax.div(xx, 2), lax.rem(xx, 2)
        rhs = jnp.concatenate(
            [
                stack([hb[core, xx, 6 * h + s, yy] for yy in range(NY) for core in range(2)])
                for s in range(6)
            ],
            axis=1,
        )
        offsets = [(2 * (4 * h + s) + hi) * 512 + 128 for s in range(4)]
        offsets += [(2 * (4 * h + 2 * s) + hi) * 512 + 256 for s in range(2)]
        lanes = pl.ds(pl.multiple_of(lo * 256, 128), 256)
        acc_out[:, lanes] += lax.dot_general(
            weights(offsets), rhs, NT, preferred_element_type=jnp.float32
        )

    def c_task(pair, h):
        rhs = jnp.concatenate(
            [
                stack(
                    [
                        hc[core, 2 * pair + yy, 2 * h + lo, s]
                        for lo in range(2) for yy in range(2) for core in range(2)
                    ]
                )
                for s in range(12)
            ],
            axis=1,
        )
        offsets = [(2 * s + h) * 512 + 384 for s in range(8)]
        offsets += [(2 * (2 * s + 1) + h) * 512 + 256 for s in range(4)]
        out = lax.dot_general(weights(offsets), rhs, NT, preferred_element_type=jnp.float32)
        for lo in range(2):
            lanes = pl.ds(pl.multiple_of(lo * 256 + pair * 128, 128), 128)
            acc_out[:, lanes] += out[:, lo * 128 : (lo + 1) * 128]

    have = {}

    def a_done(key, h, origin, ready):
        have["a", key, h] = ready
        if ("a", key, 1 - h) in have:
            def action():
                for half in (0, 1):
                    received("a", key, half)
                a_task(origin)
            push(max(ready, have["a", key, 1 - h]), action)

    def b_done(key, h, origin, ready):
        def action():
            received("b", key, h)
            b_task(origin, h)
        push(ready, action)

    def c_done(key, h, origin, ready):
        have["c", key, h] = ready
        near = [(0, 0), (1, 1), (-1, 1)]
        if key in near and all(("c", k, h) in have for k in near):
            def action():
                for k in near:
                    received("c", k, h)
                c_task(lax.div(y, 2), h)
            push(max(have["c", k, h] for k in near), action)
        if key == (0, 2):
            def action():
                received("c", key, h)
                c_task(1 - lax.div(y, 2), h)
            push(ready, action)

    def states():
        index = [next(count) for _ in range(4)]
        remote(st.at[c, y, x_lo], x_flip, index[0], send, recv)
        yield 1.5
        arrived(st.at[c, y, 1 - x_lo], index[0], recv)
        for way, k in ((1, 1), (-1, 2)):
            remote(st.at[c, y], along("y", way), index[k], send, recv)
        yield 3.0
        below, above = lax.rem(y + 3, NY), lax.rem(y + 1, NY)
        arrived(st.at[c, below], index[1], recv)
        remote(st.at[c, below], along("y", 1), index[3], send, recv)
        yield 3.1
        arrived(st.at[c, above], index[2], recv)
        yield 4.5
        arrived(st.at[c, lax.rem(y + 2, NY)], index[3], recv)
        near = next(near_count)
        remote(st.at[c], partner, near, near_send, near_recv)
        yield 6.0
        arrived(st.at[other], near, near_recv)
        tab_fill.wait()
        group = lax.div(lax.broadcasted_iota(jnp.int32, (1, 128), 1), 32)
        parts = []
        for lo in range(2):
            for pair in range(2):
                picked = st[1, 2 * pair + 1, lo, 0:1]
                for k in range(3):
                    picked = jnp.where(group == k, st[k % 2, 2 * pair + k // 2, lo, 0:1], picked)
                parts.append(picked)
        row_states = jnp.concatenate(parts, axis=1)
        marks = lax.broadcasted_iota(jnp.int32, (tab.shape[1], row_states.shape[1]), 0)
        onehot = jnp.where(marks == row_states, 1.0, 0.0).astype(jnp.bfloat16)
        allowed = jnp.dot(
            tab[...].astype(jnp.float32).astype(jnp.bfloat16), onehot, preferred_element_type=jnp.float32
        )
        acc_out[...] = jnp.where(allowed > 0.5, 0.0, LOWEST)
        w_fill.wait()

    drive(states())
    drive(
        gather(
            "c",
            [
                ("z", NZ, z, lambda p, h: hc.at[c, y, x, p if h == 0 else c_second(p)], block),
                ("x", NX, x, lambda p, h: hc.at[c, y, p, pl.ds(6 * h, 6)], 6 * block),
                ("y", NY, y, lambda p, h: c_piece(c, p, h), 24 * block),
            ],
            c_piece, 24 * block, c_done,
        )
    )
    drive(
        gather(
            "b",
            [
                ("y", NY, y, lambda p, h: hb.at[c, x, b_first(z) if h == 0 else b_second(z), p], block),
                ("z", NZ, z, lambda p, h: hb.at[c, x, b_first(p) if h == 0 else b_second(p)], 4 * block),
                ("x", NX, x, lambda p, h: b_piece(c, p, h), 24 * block),
            ],
            b_piece, 24 * block, b_done,
        )
    )
    drive(
        gather(
            "a",
            [
                ("x", NX, x, lambda p, h: ha.at[c, z, y, p, pl.ds(16 * h, 16)], block // 2),
                ("y", NY, y, lambda p, h: ha.at[c, z, p, pl.ds(2 * h, 2)], 2 * block),
                ("z", NZ, z, lambda p, h: a_piece(c, p, h), 8 * block),
            ],
            a_piece, 8 * block, a_done,
        )
    )
    while queue:
        heapq.heappop(queue)[2]()

    slots = itertools.count()

    def combine(tiles):
        peak = functools.reduce(jnp.maximum, [t[0:4] for t in tiles])
        total = sum(t[4:8] * jnp.exp(t[0:4] - peak) for t in tiles)
        return peak, total

    def put(peak, total):
        slot = ls.at[next(slots)]
        slot[0:4] = peak
        slot[4:8] = total
        return slot

    def relay(source, target, device, sends, recvs, index):
        copy = pltpu.make_async_remote_copy(
            src_ref=source, dst_ref=target, send_sem=sends.at[index],
            recv_sem=recvs.at[index], device_id=device, device_id_type=MESH,
        )
        copy.start()
        sent.append(copy)

    own = ls.at[next(slots)]
    for g in range(4):
        tile = acc_out[:, pl.ds(128 * g, 128)]
        peak = jnp.max(tile, axis=0, keepdims=True)
        own[g : g + 1] = peak
        own[4 + g : 5 + g] = jnp.sum(jnp.exp(tile - peak), axis=0, keepdims=True)
    theirs = ls.at[next(slots)]
    index = next(near_count)
    relay(own, theirs, partner, near_send, near_recv, index)
    arrived(theirs, index, near_recv)
    mine = put(*combine([own[...], theirs[...]]))
    for axis, size in (("x", NX), ("y", NY), ("z", NZ)):
        half = size // 2
        steps = [(way, d) for d in range(1, half + 1) for way in (1, -1) if d < half or way > 0]
        where = {step: (ls.at[next(slots)], next(count)) for step in steps}
        for way in (1, -1):
            target, index = where[way, 1]
            relay(mine, target, along(axis, way), send, recv, index)
        for way, d in steps:
            target, index = where[way, d]
            arrived(target, index, recv)
            if (way, d + 1) in where:
                following, index = where[way, d + 1]
                relay(target, following, along(axis, way), send, recv, index)
        peak, total = combine([mine[...]] + [where[step][0][...] for step in steps])
        if axis != "z":
            mine = put(peak, total)
    norm = peak + jnp.log(total)
    for g in range(4):
        norm_out[0:1, pl.ds(128 * g, 128)] = norm[g : g + 1]
    for copy in sent:
        copy.wait_send()


def local(hidden_rows, row_states, head_weight, grammar_table):
    depth, columns = head_weight.shape
    states = grammar_table.shape[0]
    rows = 512
    state_tile = jnp.broadcast_to(jnp.tile(row_states, 4)[None, :], (8, 128))
    anywhere = pl.BlockSpec(memory_space=pl.ANY)
    inside = pl.BlockSpec(memory_space=pltpu.VMEM)
    masked, norm = pl.pallas_call(
        kernel,
        out_shape=(
            jax.ShapeDtypeStruct((columns, rows), jnp.float32),
            jax.ShapeDtypeStruct((1, rows), jnp.float32),
        ),
        in_specs=[anywhere] * 4,
        out_specs=(inside, inside),
        scratch_shapes=[
            pltpu.VMEM((2, NZ, NY, NX, 32, 128), jnp.bfloat16),
            pltpu.VMEM((2, NX, 16, NY, 32, 128), jnp.bfloat16),
            pltpu.VMEM((2, NY, NX, 16, 32, 128), jnp.bfloat16),
            pltpu.VMEM((2, NY, 2, 8, 128), jnp.int32),
            pltpu.VMEM((columns, depth), jnp.bfloat16),
            pltpu.VMEM((columns, states), jnp.int32),
            pltpu.VMEM((24, 8, 128), jnp.float32),
            pltpu.SemaphoreType.DMA((100,)),
            pltpu.SemaphoreType.DMA((100,)),
            pltpu.SemaphoreType.DMA((36,)),
            pltpu.SemaphoreType.DMA((36,)),
            pltpu.SemaphoreType.DMA((8,)),
        ],
        compiler_params=pltpu.CompilerParams(
            collective_id=0, has_side_effects=True, vmem_limit_bytes=56 << 20
        ),
    )(hidden_rows, state_tile, head_weight.T, grammar_table.T)
    log_probs = jnp.where(masked > 0.5 * LOWEST, masked - norm, 0.0)
    return (log_probs.T, norm[0])


def solution(mesh):
    placed = (
        P("vocab", "rows"),
        P("vocab"),
        P(None, ("rows", "vocab")),
        P(None, ("rows", "vocab")),
    )
    return jax.shard_map(
        local,
        mesh=mesh,
        in_specs=placed,
        out_specs=(P(None, ("rows", "vocab")), P()),
        check_vma=False,
    )
```

```python
import heapq
import itertools

import jax
import jax.numpy as jnp
from jax import lax
from jax.experimental import pallas as pl
from jax.experimental.pallas import tpu as pltpu
from jax.sharding import PartitionSpec as P

LOWEST = -1e30
NX, NY, NZ = 4, 4, 8
MESH = pl.DeviceIdType.MESH
NT = (((1,), (1,)), ((), ()))
FIRST_HOP, NEXT_HOP, LINK, NEAR_HOP, NEAR = 2.7, 0.6, 46e3, 1.0, 2e5
A_TASK, G_TASK = 0.4, 0.5


def place(x, y, z, c):
    rows = z * 2 + lax.div(x, 2)
    vocab = lax.rem(x, 2) * 8 + y * 2 + c
    return (rows, vocab)


def shifted(pos, step, size):
    return lax.rem(pos + size + step, size)


def short(step, size):
    return min(step % size, -step % size)


PLANE = sorted(
    [(i, j) for i in range(NX) for j in range(NY) if (i, j) != (0, 0)],
    key=lambda s: -short(s[0], NX) - short(s[1], NY),
)
PLANE_CORES = [(0, 0, 1)] + [(i, j, k) for i, j in PLANE for k in range(2)]
PLANE_CORES = PLANE_CORES[1:] + PLANE_CORES[:1]
COLUMN = sorted(range(1, NZ), key=lambda s: -short(s, NZ))


def kernel(
    hid, st_in, w_in, tab_in, acc_out, norm_out,
    ha, g, st, w, tab, ls, send, recv, near_send, near_recv, bulk_send, bulk_recv, local,
):
    r, v = lax.axis_index("rows"), lax.axis_index("vocab")
    z, x = lax.div(r, 2), lax.rem(r, 2) * 2 + lax.div(v, 8)
    y, c = lax.rem(lax.div(v, 2), NY), lax.rem(v, 2)
    other = 1 - c
    sizes = {"x": NX, "y": NY, "z": NZ}
    here = {"x": x, "y": y, "z": z}

    def away(dx=0, dy=0, dz=0, dc=0):
        return place(
            shifted(x, dx, NX), shifted(y, dy, NY), shifted(z, dz, NZ), c if dc == 0 else other
        )

    x_lo = lax.rem(x, 2)
    q2_slot = jnp.where(lax.rem(z, 2) == 0, 8, 20) + lax.div(z, 2)
    own_slots = (z, q2_slot, 12 + z)

    fills = []

    def fill(source, target):
        copy = pltpu.make_async_copy(source, target, local.at[len(fills)])
        copy.start()
        fills.append(copy)
        return copy

    quarter = [hid.at[:, pl.ds(128 * q, 128)] for q in range(4)]
    for q, slot in zip((1, 2, 3), own_slots):
        fill(quarter[q], g.at[c, x, y, slot])
    fill(quarter[0], ha.at[c, z, y, x])
    fill(st_in, st.at[x_lo, y, c])
    tab_fill = fill(tab_in, tab)
    w_fill = fill(w_in, w)

    barrier = pltpu.get_barrier_semaphore()
    friends = [away(i, j, 0, k) for i, j, k in PLANE_CORES] + [away(dz=s) for s in COLUMN]
    for friend in friends:
        pl.semaphore_signal(barrier, inc=1, device_id=friend, device_id_type=MESH)
    pl.semaphore_wait(barrier, len(friends))
    for copy in fills[:5]:
        copy.wait()

    count, near_count = itertools.count(), itertools.count()
    sent = []

    def remote(source, target, device, send_sem, recv_sem):
        copy = pltpu.make_async_remote_copy(
            src_ref=source, dst_ref=target, send_sem=send_sem, recv_sem=recv_sem,
            device_id=device, device_id_type=MESH,
        )
        copy.start()
        return copy

    def arrived(target, sem):
        pltpu.make_async_copy(target, target, sem).wait()

    clock = [0.0]
    queue = []
    order = itertools.count()
    links = {}

    def post(time, action, rank=0):
        heapq.heappush(queue, (time, rank, next(order), action))

    def through(link, nbytes, rate, latency):
        links[link] = max(clock[0], links.get(link, 0.0)) + nbytes / rate
        return links[link] + latency

    for s in COLUMN:
        for slot in own_slots:
            block = g.at[c, x, y, slot]
            remote(block, block, away(dz=s), bulk_send.at[0], bulk_recv.at[0])
    own_tile = st.at[x_lo, y, c]
    for i, j in PLANE:
        block = ha.at[c, z, y, x]
        remote(block, block, away(i, j), bulk_send.at[1], bulk_recv.at[1])
    x_other = 1 - 2 * x_lo
    for lo in (1, 0):
        for j in range(NY):
            for k in range(2):
                if (lo, j, k) != (0, 0, 0):
                    device = place(
                        x + x_other if lo else x, shifted(y, j, NY), z, c if k == 0 else other
                    )
                    remote(own_tile, own_tile, device, bulk_send.at[2], bulk_recv.at[2])

    done = set()
    near_at = {}
    tasks = []

    def near_landed(unit):
        done.add(unit)
        for task in list(tasks):
            needs, action = task
            if all(n in done for n in needs):
                tasks.remove(task)
                post(clock[0], action, 1)

    def hand_over(unit, piece, nbytes):
        index = next(near_count)
        source = piece(c)
        sent.append(remote(source, source, away(dc=1), near_send.at[index], near_recv.at[index]))
        near_at[unit] = (piece(other), index)
        post(through("near", nbytes, NEAR, NEAR_HOP), lambda: near_landed(unit))

    def take(units):
        for unit in units:
            if unit in near_at:
                target, index = near_at.pop(unit)
                arrived(target, near_recv.at[index])

    def spread(axis, way, d, h, pieces, piece, nbytes, seen):
        size = sizes[axis]
        half = size // 2
        index = next(count)
        source = piece(shifted(here[axis], -way * (d - 1), size), h)
        device = away(**{"d" + axis: way})
        sent.append(remote(source, source, device, send.at[index], recv.at[index]))

        def land():
            origin = shifted(here[axis], -way * d, size)
            arrived(piece(origin, h), recv.at[index])
            final = h < pieces // 2 if way > 0 else h >= pieces // 2
            if d + 1 < half or (d + 1 == half and final):
                spread(axis, way, d + 1, h, pieces, piece, nbytes, seen)
            seen(-way * d if d < half else half, origin, h)

        post(through((axis, way), nbytes, LINK, FIRST_HOP), land)

    def around(axis, pieces, piece, nbytes, seen):
        for i in range(pieces):
            spread(axis, 1, 1, i, pieces, piece, nbytes, seen)
            spread(axis, -1, 1, pieces - 1 - i, pieces, piece, nbytes, seen)

    block_bytes = 32 * 128 * 2
    unit_bytes = 6 * block_bytes

    def unit_piece(xx, yy, k):
        return lambda core: g.at[core, xx, yy, pl.ds(6 * k, 6)]

    def column_ready():
        arrived(g.at[c, x, y, pl.ds(0, 21)], bulk_recv.at[0])

        def colour(first, last, ks):
            def at(p_first, p_last, k):
                where = {first: p_first, last: p_last}
                return unit_piece(where["x"], where["y"], k)

            def onward(rel_first, p_first, h):
                k = ks[h]

                def seen(rel_last, p_last, _):
                    rel = {first: rel_first, last: rel_last}
                    hand_over((rel["x"], rel["y"], k), at(p_first, p_last, k), unit_bytes)

                for way in (1, -1):
                    spread(
                        last, way, 1, h, 2, lambda p, hh: at(p_first, p, ks[hh])(c), unit_bytes, seen
                    )

            def seen_first(rel_first, p_first, h):
                onward(rel_first, p_first, h)
                rel = {first: rel_first, last: 0}
                hand_over((rel["x"], rel["y"], ks[h]), at(p_first, here[last], ks[h]), unit_bytes)

            return (
                lambda: around(
                    first, 2, lambda p, h: at(p, here[last], ks[h])(c), unit_bytes, seen_first
                ),
                lambda: [onward(0, here[first], h) for h in range(2)],
            )

        b_first, b_last = colour("y", "x", (0, 1))
        c_first, c_last = colour("x", "y", (2, 3))
        b_first()
        c_first()
        b_last()
        c_last()
        for k in range(4):
            hand_over((0, 0, k), unit_piece(x, y, k), unit_bytes)

    def plane_ready():
        arrived(g.at[c, x, y, pl.ds(0, 15)], bulk_recv.at[1])
        piece = lambda core, p, h: ha.at[core, p, h]

        def seen(rel, p, h):
            hand_over(("a", rel, h), lambda core: piece(core, p, h), 4 * block_bytes)

        around("z", 4, lambda p, h: piece(c, p, h), 4 * block_bytes, seen)
        hand_over(("a", 0, 0), lambda core: ha.at[core, z], 16 * block_bytes)

    def weights(offsets):
        return jnp.concatenate(
            [w[:, pl.ds(pl.multiple_of(o, 128), 128)] for o in offsets], axis=1
        )

    def stack(parts):
        return jnp.concatenate(parts, axis=0)

    def a_task(zz):
        rhs = jnp.concatenate(
            [
                stack(
                    [
                        ha[core, zz, yy, 2 * hi + lo]
                        for lo in range(2) for yy in range(NY) for core in range(2)
                    ]
                )
                for hi in range(2)
            ],
            axis=1,
        )
        lhs = weights([(2 * zz + hi) * 512 for hi in range(2)])
        acc_out[...] += lax.dot_general(lhs, rhs, NT, preferred_element_type=jnp.float32)

    def column_of(slot, hi):
        if slot < 8:
            return (2 * slot + hi) * 512 + 128
        if slot < 12:
            return (4 * (slot - 8) + hi) * 512 + 256
        if slot < 20:
            return (2 * (slot - 12) + hi) * 512 + 384
        return (4 * (slot - 20) + 2 + hi) * 512 + 256

    def b_task(xx, k):
        hi, lo = lax.div(xx, 2), lax.rem(xx, 2)
        slots = range(6 * k, 6 * k + 6)
        rhs = jnp.concatenate(
            [stack([g[core, xx, yy, s] for yy in range(NY) for core in range(2)]) for s in slots],
            axis=1,
        )
        lanes = pl.ds(pl.multiple_of(lo * 256, 128), 256)
        acc_out[:, lanes] += lax.dot_general(
            weights([column_of(s, hi) for s in slots]), rhs, NT, preferred_element_type=jnp.float32
        )

    def c_task(hi, pair, k):
        slots = range(6 * k, 6 * k + 6)
        rhs = jnp.concatenate(
            [
                stack(
                    [
                        g[core, 2 * hi + lo, 2 * pair + yy, s]
                        for lo in range(2) for yy in range(2) for core in range(2)
                    ]
                )
                for s in slots
            ],
            axis=1,
        )
        out = lax.dot_general(
            weights([column_of(s, hi) for s in slots]), rhs, NT, preferred_element_type=jnp.float32
        )
        for lo in range(2):
            lanes = pl.ds(pl.multiple_of(lo * 256 + pair * 128, 128), 128)
            acc_out[:, lanes] += out[:, lo * 128 : (lo + 1) * 128]

    def add_task(needs, cost, work):
        def action():
            take(needs)
            work()
            clock[0] += cost

        tasks.append((needs, action))

    for rel in (0, 1, -1, 2, -2, 3, -3, 4):
        needs = [("a", rel, h) for h in range(4)] if rel else [("a", 0, 0)]
        add_task(
            ["start"] + needs, A_TASK, lambda rel=rel: a_task(shifted(z, rel, NZ))
        )
    for rel in (0, 1, -1, 2):
        for k in (0, 1):
            add_task(
                ["start"] + [(rel, dy, k) for dy in (0, 1, -1, 2)], G_TASK,
                lambda rel=rel, k=k: b_task(shifted(x, rel, NX), k),
            )
    close, far = (0, 1, -1), (1, -1, 2)
    for dxs in (close, far):
        for dys in (close, far):
            for k in (2, 3):
                add_task(
                    ["start"] + [(dx, dy, k) for dx in dxs for dy in dys], G_TASK,
                    lambda dxs=dxs, dys=dys, k=k: c_task(
                        lax.div(x, 2) if dxs is close else 1 - lax.div(x, 2),
                        lax.div(y, 2) if dys is close else 1 - lax.div(y, 2),
                        k,
                    ),
                )

    def begin():
        arrived(ls.at[pl.ds(1, 15)], bulk_recv.at[2])
        tab_fill.wait()
        group = lax.div(lax.broadcasted_iota(jnp.int32, (1, 128), 1), 32)
        parts = []
        for lo in range(2):
            for pair in range(2):
                picked = st[lo, 2 * pair + 1, 1, 0:1]
                for k in range(3):
                    picked = jnp.where(group == k, st[lo, 2 * pair + k // 2, k % 2, 0:1], picked)
                parts.append(picked)
        row_states = jnp.concatenate(parts, axis=1)
        marks = lax.broadcasted_iota(jnp.int32, (tab.shape[1], row_states.shape[1]), 0)
        onehot = jnp.where(marks == row_states, 1.0, 0.0).astype(jnp.bfloat16)
        allowed = jnp.dot(
            tab[...].astype(jnp.float32).astype(jnp.bfloat16), onehot, preferred_element_type=jnp.float32
        )
        acc_out[...] = jnp.where(allowed > 0.5, 0.0, LOWEST)
        w_fill.wait()
        clock[0] += 1.0
        near_landed("start")

    post(6.0, plane_ready)
    post(7.0, column_ready)
    post(7.5, begin)
    while queue:
        time, _, _, action = heapq.heappop(queue)
        clock[0] = max(clock[0], time)
        action()

    own = ls.at[0]
    for k in range(4):
        tile = acc_out[:, pl.ds(128 * k, 128)]
        peak = jnp.max(tile, axis=0, keepdims=True)
        own[k : k + 1] = peak
        own[4 + k : 5 + k] = jnp.sum(jnp.exp(tile - peak), axis=0, keepdims=True)

    def combine(first, number):
        peaks, totals = ls[first : first + number, 0:4], ls[first : first + number, 4:8]
        peak = jnp.max(peaks, axis=0)
        return peak, jnp.sum(totals * jnp.exp(peaks - peak[None]), axis=0)

    for n, (i, j, k) in enumerate(PLANE_CORES):
        remote(own, ls.at[1 + n], away(i, j, 0, k), bulk_send.at[3], bulk_recv.at[3])
    arrived(ls.at[pl.ds(1, 31)], bulk_recv.at[3])
    mine = ls.at[32]
    mine[0:4], mine[4:8] = combine(0, 32)
    for n, s in enumerate(COLUMN):
        remote(mine, ls.at[33 + n], away(dz=s), bulk_send.at[4], bulk_recv.at[4])
    arrived(ls.at[pl.ds(33, 7)], bulk_recv.at[4])
    peak, total = combine(32, 8)
    norm = peak + jnp.log(total)
    for k in range(4):
        norm_out[0:1, pl.ds(128 * k, 128)] = norm[k : k + 1]

    for copy in sent:
        copy.wait_send()
    arrived(g.at[c, x, y, pl.ds(0, 21)], bulk_send.at[0])
    arrived(g.at[c, x, y, pl.ds(0, 15)], bulk_send.at[1])
    arrived(ls.at[pl.ds(1, 15)], bulk_send.at[2])
    arrived(ls.at[pl.ds(1, 31)], bulk_send.at[3])
    arrived(ls.at[pl.ds(33, 7)], bulk_send.at[4])


def local(hidden_rows, row_states, head_weight, grammar_table):
    depth, columns = head_weight.shape
    states = grammar_table.shape[0]
    rows = 512
    state_tile = jnp.broadcast_to(jnp.tile(row_states, 4)[None, :], (8, 128))
    anywhere = pl.BlockSpec(memory_space=pl.ANY)
    inside = pl.BlockSpec(memory_space=pltpu.VMEM)
    masked, norm = pl.pallas_call(
        kernel,
        out_shape=(
            jax.ShapeDtypeStruct((columns, rows), jnp.float32),
            jax.ShapeDtypeStruct((1, rows), jnp.float32),
        ),
        in_specs=[anywhere] * 4,
        out_specs=(inside, inside),
        scratch_shapes=[
            pltpu.VMEM((2, NZ, NY, NX, 32, 128), jnp.bfloat16),
            pltpu.VMEM((2, NX, NY, 24, 32, 128), jnp.bfloat16),
            pltpu.VMEM((2, NY, 2, 8, 128), jnp.int32),
            pltpu.VMEM((columns, depth), jnp.bfloat16),
            pltpu.VMEM((columns, states), jnp.int32),
            pltpu.VMEM((40, 8, 128), jnp.float32),
            pltpu.SemaphoreType.DMA((92,)),
            pltpu.SemaphoreType.DMA((92,)),
            pltpu.SemaphoreType.DMA((96,)),
            pltpu.SemaphoreType.DMA((96,)),
            pltpu.SemaphoreType.DMA((5,)),
            pltpu.SemaphoreType.DMA((5,)),
            pltpu.SemaphoreType.DMA((8,)),
        ],
        compiler_params=pltpu.CompilerParams(
            collective_id=0, has_side_effects=True, vmem_limit_bytes=56 << 20
        ),
    )(hidden_rows, state_tile, head_weight.T, grammar_table.T)
    log_probs = jnp.where(masked > 0.5 * LOWEST, masked - norm, 0.0)
    return (log_probs.T, norm[0])


def solution(mesh):
    placed = (
        P("vocab", "rows"),
        P("vocab"),
        P(None, ("rows", "vocab")),
        P(None, ("rows", "vocab")),
    )
    return jax.shard_map(
        local,
        mesh=mesh,
        in_specs=placed,
        out_specs=(P(None, ("rows", "vocab")), P()),
        check_vma=False,
    )
```

```python
import heapq
import itertools

import jax
import jax.numpy as jnp
from jax import lax
from jax.experimental import pallas as pl
from jax.experimental.pallas import tpu as pltpu
from jax.sharding import PartitionSpec as P

LOWEST = -1e30
NX, NY, NZ = 4, 4, 8
MESH = pl.DeviceIdType.MESH
NT = (((1,), (1,)), ((), ()))
FIRST_HOP, NEXT_HOP, LINK, NEAR_HOP, NEAR = 2.3, 0.6, 90e3, 1.0, 6e5
A_TASK, G_TASK = 0.2, 0.4


def place(x, y, z, c):
    rows = z * 2 + lax.div(x, 2)
    vocab = lax.rem(x, 2) * 8 + y * 2 + c
    return (rows, vocab)


def shifted(pos, step, size):
    return lax.rem(pos + size + step, size)


def short(step, size):
    return min(step % size, -step % size)


PLANE = sorted(
    [(i, j) for i in range(NX) for j in range(NY) if (i, j) != (0, 0)],
    key=lambda s: -short(s[0], NX) - short(s[1], NY),
)
PLANE_CORES = [(0, 0, 1)] + [(i, j, k) for i, j in PLANE for k in range(2)]
PLANE_CORES = PLANE_CORES[1:] + PLANE_CORES[:1]
COLUMN = sorted(range(1, NZ), key=lambda s: -short(s, NZ))


def kernel(
    hid, st_in, w_in, tab_in, acc_out, norm_out,
    ha, g, st, raw, w, tab, ls, send, recv, near_send, near_recv, bulk_send, bulk_recv, local,
):
    r, v = lax.axis_index("rows"), lax.axis_index("vocab")
    z, x = lax.div(r, 2), lax.rem(r, 2) * 2 + lax.div(v, 8)
    y, c = lax.rem(lax.div(v, 2), NY), lax.rem(v, 2)
    other = 1 - c
    sizes = {"x": NX, "y": NY, "z": NZ}
    here = {"x": x, "y": y, "z": z}

    def away(dx=0, dy=0, dz=0, dc=0):
        return place(
            shifted(x, dx, NX), shifted(y, dy, NY), shifted(z, dz, NZ), c if dc == 0 else other
        )

    x_lo = lax.rem(x, 2)
    q2_slot = jnp.where(lax.rem(z, 2) == 0, 8, 20) + lax.div(z, 2)
    own_slots = (z, q2_slot, 12 + z)

    fills = []

    def fill(source, target):
        copy = pltpu.make_async_copy(source, target, local.at[len(fills)])
        copy.start()
        fills.append(copy)
        return copy

    quarter = [hid.at[:, pl.ds(128 * q, 128)] for q in range(4)]
    for q, slot in zip((1, 2, 3), own_slots):
        fill(quarter[q], g.at[c, x, y, slot])
    fill(quarter[0], ha.at[c, z, y, x])
    fill(st_in, raw)
    tab_fill = fill(tab_in, tab)
    w_fill = fill(w_in, w)

    barrier = pltpu.get_barrier_semaphore()
    friends = [away(i, j, 0, k) for i, j, k in PLANE_CORES] + [away(dz=s) for s in COLUMN]
    for friend in friends:
        pl.semaphore_signal(barrier, inc=1, device_id=friend, device_id_type=MESH)
    pl.semaphore_wait(barrier, len(friends))
    for copy in fills[:5]:
        copy.wait()
    st[x_lo, y, c] = jnp.broadcast_to(jnp.concatenate([raw[...]] * 4, axis=1), (8, 128))

    count, near_count = itertools.count(), itertools.count()
    sent = []

    def remote(source, target, device, send_sem, recv_sem):
        copy = pltpu.make_async_remote_copy(
            src_ref=source, dst_ref=target, send_sem=send_sem, recv_sem=recv_sem,
            device_id=device, device_id_type=MESH,
        )
        copy.start()
        return copy

    def arrived(target, sem):
        pltpu.make_async_copy(target, target, sem).wait()

    clock = [0.0]
    queue = []
    order = itertools.count()
    links = {}

    def post(time, action, rank=0):
        heapq.heappush(queue, (time, rank, next(order), action))

    def through(link, nbytes, rate, latency):
        links[link] = max(clock[0], links.get(link, 0.0)) + nbytes / rate
        return links[link] + latency

    for s in COLUMN:
        for slot in own_slots:
            block = g.at[c, x, y, slot]
            remote(block, block, away(dz=s), bulk_send.at[0], bulk_recv.at[0])
    own_tile = st.at[x_lo, y, c]
    for i, j in PLANE:
        block = ha.at[c, z, y, x]
        remote(block, block, away(i, j), bulk_send.at[1], bulk_recv.at[1])
    x_other = 1 - 2 * x_lo
    for lo in (1, 0):
        for j in range(NY):
            for k in range(2):
                if (lo, j, k) != (0, 0, 0):
                    device = place(
                        x + x_other if lo else x, shifted(y, j, NY), z, c if k == 0 else other
                    )
                    remote(own_tile, own_tile, device, bulk_send.at[2], bulk_recv.at[2])

    done = set()
    near_at = {}
    tasks = []

    def near_landed(unit):
        done.add(unit)
        for task in list(tasks):
            needs, action = task
            if all(n in done for n in needs):
                tasks.remove(task)
                post(clock[0], action, 1)

    def hand_over(unit, piece, nbytes):
        index = next(near_count)
        source = piece(c)
        sent.append(remote(source, source, away(dc=1), near_send.at[index], near_recv.at[index]))
        near_at[unit] = (piece(other), index)
        post(through("near", nbytes, NEAR, NEAR_HOP), lambda: near_landed(unit))

    def take(units):
        for unit in units:
            if unit in near_at:
                target, index = near_at.pop(unit)
                arrived(target, near_recv.at[index])

    def spread(axis, way, d, h, pieces, piece, nbytes, seen):
        size = sizes[axis]
        half = size // 2
        index = next(count)
        source = piece(shifted(here[axis], -way * (d - 1), size), h)
        device = away(**{"d" + axis: way})
        sent.append(remote(source, source, device, send.at[index], recv.at[index]))

        def land():
            origin = shifted(here[axis], -way * d, size)
            arrived(piece(origin, h), recv.at[index])
            final = h < pieces // 2 if way > 0 else h >= pieces // 2
            if d + 1 < half or (d + 1 == half and final):
                spread(axis, way, d + 1, h, pieces, piece, nbytes, seen)
            seen(-way * d if d < half else half, origin, h)

        post(through((axis, way), nbytes, LINK, FIRST_HOP), land)

    def around(axis, pieces, piece, nbytes, seen):
        for i in range(pieces):
            spread(axis, 1, 1, i, pieces, piece, nbytes, seen)
            spread(axis, -1, 1, pieces - 1 - i, pieces, piece, nbytes, seen)

    block_bytes = 32 * 128 * 2
    unit_bytes = 6 * block_bytes

    def unit_piece(xx, yy, k):
        return lambda core: g.at[core, xx, yy, pl.ds(6 * k, 6)]

    def column_ready():
        arrived(g.at[c, x, y, pl.ds(0, 21)], bulk_recv.at[0])

        def colour(first, last, ks):
            def at(p_first, p_last, k):
                where = {first: p_first, last: p_last}
                return unit_piece(where["x"], where["y"], k)

            def onward(rel_first, p_first, h):
                k = ks[h]

                def seen(rel_last, p_last, _):
                    rel = {first: rel_first, last: rel_last}
                    hand_over((rel["x"], rel["y"], k), at(p_first, p_last, k), unit_bytes)

                for way in (1, -1):
                    spread(
                        last, way, 1, h, 2, lambda p, hh: at(p_first, p, ks[hh])(c), unit_bytes, seen,
                    )

            def seen_first(rel_first, p_first, h):
                onward(rel_first, p_first, h)
                rel = {first: rel_first, last: 0}
                hand_over((rel["x"], rel["y"], ks[h]), at(p_first, here[last], ks[h]), unit_bytes)

            return (
                lambda: around(
                    first, 2, lambda p, h: at(p, here[last], ks[h])(c), unit_bytes, seen_first
                ),
                lambda: [onward(0, here[first], h) for h in range(2)],
            )

        b_first, b_last = colour("y", "x", (0, 1))
        c_first, c_last = colour("x", "y", (2, 3))
        b_first()
        c_first()
        b_last()
        c_last()
        for k in range(4):
            hand_over((0, 0, k), unit_piece(x, y, k), unit_bytes)

    def plane_ready():
        arrived(g.at[c, x, y, pl.ds(0, 15)], bulk_recv.at[1])
        piece = lambda core, p, h: ha.at[core, p, pl.ds(2 * h, 2)]

        def seen(rel, p, h):
            hand_over(("a", rel, h), lambda core: piece(core, p, h), 8 * block_bytes)

        around("z", 2, lambda p, h: piece(c, p, h), 8 * block_bytes, seen)
        hand_over(("a", 0, 0), lambda core: ha.at[core, z], 16 * block_bytes)

    def weights(offsets):
        return jnp.concatenate(
            [w[:, pl.ds(pl.multiple_of(o, 128), 128)] for o in offsets], axis=1
        )

    def stack(parts):
        return jnp.concatenate(parts, axis=0)

    def a_task(zz):
        rhs = jnp.concatenate(
            [
                stack(
                    [
                        ha[core, zz, yy, 2 * hi + lo]
                        for lo in range(2) for yy in range(NY) for core in range(2)
                    ]
                )
                for hi in range(2)
            ],
            axis=1,
        )
        lhs = weights([(2 * zz + hi) * 512 for hi in range(2)])
        acc_out[...] += lax.dot_general(lhs, rhs, NT, preferred_element_type=jnp.float32)

    def column_of(slot, hi):
        if slot < 8:
            return (2 * slot + hi) * 512 + 128
        if slot < 12:
            return (4 * (slot - 8) + hi) * 512 + 256
        if slot < 20:
            return (2 * (slot - 12) + hi) * 512 + 384
        return (4 * (slot - 20) + 2 + hi) * 512 + 256

    def b_task(xx, k):
        hi, lo = lax.div(xx, 2), lax.rem(xx, 2)
        slots = range(6 * k, 6 * k + 6)
        rhs = jnp.concatenate(
            [stack([g[core, xx, yy, s] for yy in range(NY) for core in range(2)]) for s in slots],
            axis=1,
        )
        lanes = pl.ds(pl.multiple_of(lo * 256, 128), 256)
        acc_out[:, lanes] += lax.dot_general(
            weights([column_of(s, hi) for s in slots]), rhs, NT, preferred_element_type=jnp.float32
        )

    def c_task(hi, pair, k):
        slots = range(6 * k, 6 * k + 6)
        rhs = jnp.concatenate(
            [
                stack(
                    [
                        g[core, 2 * hi + lo, 2 * pair + yy, s]
                        for lo in range(2) for yy in range(2) for core in range(2)
                    ]
                )
                for s in slots
            ],
            axis=1,
        )
        out = lax.dot_general(
            weights([column_of(s, hi) for s in slots]), rhs, NT, preferred_element_type=jnp.float32
        )
        for lo in range(2):
            lanes = pl.ds(pl.multiple_of(lo * 256 + pair * 128, 128), 128)
            acc_out[:, lanes] += out[:, lo * 128 : (lo + 1) * 128]

    def add_task(needs, cost, work):
        def action():
            take(needs)
            work()
            clock[0] += cost

        tasks.append((needs, action))

    for rel in (0, 1, -1, 2, -2, 3, -3, 4):
        needs = [("a", rel, h) for h in range(2)] if rel else [("a", 0, 0)]
        add_task(
            ["start"] + needs, A_TASK, lambda rel=rel: a_task(shifted(z, rel, NZ))
        )
    for rel in (0, 1, -1, 2):
        for k in (0, 1):
            add_task(
                ["start"] + [(rel, dy, k) for dy in (0, 1, -1, 2)], G_TASK,
                lambda rel=rel, k=k: b_task(shifted(x, rel, NX), k),
            )
    close, far = (0, 1, -1), (1, -1, 2)
    for dxs in (close, far):
        for dys in (close, far):
            for k in (2, 3):
                add_task(
                    ["start"] + [(dx, dy, k) for dx in dxs for dy in dys], G_TASK,
                    lambda dxs=dxs, dys=dys, k=k: c_task(
                        lax.div(x, 2) if dxs is close else 1 - lax.div(x, 2),
                        lax.div(y, 2) if dys is close else 1 - lax.div(y, 2),
                        k,
                    ),
                )

    def begin():
        arrived(ls.at[pl.ds(1, 15)], bulk_recv.at[2])
        tab_fill.wait()
        group = lax.div(lax.broadcasted_iota(jnp.int32, (1, 128), 1), 32)
        parts = []
        for lo in range(2):
            for pair in range(2):
                picked = st[lo, 2 * pair + 1, 1, 0:1]
                for k in range(3):
                    picked = jnp.where(group == k, st[lo, 2 * pair + k // 2, k % 2, 0:1], picked)
                parts.append(picked)
        row_states = jnp.concatenate(parts, axis=1)
        marks = lax.broadcasted_iota(jnp.int32, (tab.shape[1], row_states.shape[1]), 0)
        onehot = jnp.where(marks == row_states, 1.0, 0.0).astype(jnp.bfloat16)
        allowed = jnp.dot(
            tab[...].astype(jnp.float32).astype(jnp.bfloat16), onehot, preferred_element_type=jnp.float32
        )
        acc_out[...] = jnp.where(allowed > 0.5, 0.0, LOWEST)
        w_fill.wait()
        clock[0] += 1.0
        near_landed("start")

    post(6.0, plane_ready)
    post(7.0, column_ready)
    post(6.5, begin)
    while queue:
        time, _, _, action = heapq.heappop(queue)
        clock[0] = max(clock[0], time)
        action()

    own = ls.at[0]
    for k in range(4):
        tile = acc_out[:, pl.ds(128 * k, 128)]
        peak = jnp.max(tile, axis=0, keepdims=True)
        own[k : k + 1] = peak
        own[4 + k : 5 + k] = jnp.sum(jnp.exp(tile - peak), axis=0, keepdims=True)

    def combine(first, number):
        peaks, totals = ls[first : first + number, 0:4], ls[first : first + number, 4:8]
        peak = jnp.max(peaks, axis=0)
        return peak, jnp.sum(totals * jnp.exp(peaks - peak[None]), axis=0)

    for n, (i, j, k) in enumerate(PLANE_CORES):
        remote(own, ls.at[1 + n], away(i, j, 0, k), bulk_send.at[3], bulk_recv.at[3])
    arrived(ls.at[pl.ds(1, 31)], bulk_recv.at[3])
    mine = ls.at[32]
    mine[0:4], mine[4:8] = combine(0, 32)
    for n, s in enumerate(COLUMN):
        remote(mine, ls.at[33 + n], away(dz=s), bulk_send.at[4], bulk_recv.at[4])
    arrived(ls.at[pl.ds(33, 7)], bulk_recv.at[4])
    peak, total = combine(32, 8)
    norm = peak + jnp.log(total)
    for k in range(4):
        norm_out[0:1, pl.ds(128 * k, 128)] = norm[k : k + 1]

    for copy in sent:
        copy.wait_send()
    arrived(g.at[c, x, y, pl.ds(0, 21)], bulk_send.at[0])
    arrived(g.at[c, x, y, pl.ds(0, 15)], bulk_send.at[1])
    arrived(ls.at[pl.ds(1, 15)], bulk_send.at[2])
    arrived(ls.at[pl.ds(1, 31)], bulk_send.at[3])
    arrived(ls.at[pl.ds(33, 7)], bulk_send.at[4])


def local(hidden_rows, row_states, head_weight, grammar_table):
    depth, columns = head_weight.shape
    states = grammar_table.shape[0]
    rows = 512
    operands = (hidden_rows, row_states[None, :], head_weight.T, grammar_table.T)
    anywhere = pl.BlockSpec(memory_space=pl.ANY)
    inside = pl.BlockSpec(memory_space=pltpu.VMEM)
    masked, norm = pl.pallas_call(
        kernel,
        out_shape=(
            jax.ShapeDtypeStruct((columns, rows), jnp.float32),
            jax.ShapeDtypeStruct((1, rows), jnp.float32),
        ),
        in_specs=[anywhere] * 4,
        out_specs=(inside, inside),
        scratch_shapes=[
            pltpu.VMEM((2, NZ, NY, NX, 32, 128), jnp.bfloat16),
            pltpu.VMEM((2, NX, NY, 24, 32, 128), jnp.bfloat16),
            pltpu.VMEM((2, NY, 2, 8, 128), jnp.int32),
            pltpu.VMEM((1, 32), jnp.int32),
            pltpu.VMEM((columns, depth), jnp.bfloat16),
            pltpu.VMEM((columns, states), jnp.int32),
            pltpu.VMEM((40, 8, 128), jnp.float32),
            pltpu.SemaphoreType.DMA((92,)),
            pltpu.SemaphoreType.DMA((92,)),
            pltpu.SemaphoreType.DMA((96,)),
            pltpu.SemaphoreType.DMA((96,)),
            pltpu.SemaphoreType.DMA((5,)),
            pltpu.SemaphoreType.DMA((5,)),
            pltpu.SemaphoreType.DMA((8,)),
        ],
        compiler_params=pltpu.CompilerParams(
            collective_id=0, has_side_effects=True, vmem_limit_bytes=40 << 20
        ),
    )(*(pltpu.with_memory_space_constraint(a, pltpu.HBM) for a in operands))
    log_probs = jnp.where(masked > 0.5 * LOWEST, masked - norm, 0.0)
    return (log_probs.T, norm[0])


def solution(mesh):
    placed = (
        P("vocab", "rows"),
        P("vocab"),
        P(None, ("rows", "vocab")),
        P(None, ("rows", "vocab")),
    )
    return jax.shard_map(
        local,
        mesh=mesh,
        in_specs=placed,
        out_specs=(P(None, ("rows", "vocab")), P()),
        check_vma=False,
    )
```

```python
import heapq
import itertools

import jax
import jax.numpy as jnp
from jax import lax
from jax.experimental import pallas as pl
from jax.experimental.pallas import tpu as pltpu
from jax.sharding import PartitionSpec as P

LOWEST = -1e30
NX, NY, NZ = 4, 4, 8
MESH = pl.DeviceIdType.MESH
NT = (((1,), (1,)), ((), ()))
FIRST_HOP, NEXT_HOP, LINK, NEAR_HOP, NEAR = 2.3, 0.6, 90e3, 1.0, 6e5
A_TASK, G_TASK = 0.2, 0.4


def place(x, y, z, c):
    rows = z * 2 + lax.div(x, 2)
    vocab = lax.rem(x, 2) * 8 + y * 2 + c
    return (rows, vocab)


def shifted(pos, step, size):
    return lax.rem(pos + size + step, size)


def short(step, size):
    return min(step % size, -step % size)


PLANE = sorted(
    [(i, j) for i in range(NX) for j in range(NY) if (i, j) != (0, 0)],
    key=lambda s: -short(s[0], NX) - short(s[1], NY),
)
PLANE_CORES = [(0, 0, 1)] + [(i, j, k) for i, j in PLANE for k in range(2)]
PLANE_CORES = PLANE_CORES[1:] + PLANE_CORES[:1]
COLUMN = sorted(range(1, NZ), key=lambda s: -short(s, NZ))


def kernel(
    hid, st_in, w_in, tab_in, acc_out, norm_out,
    ha, g, st, raw, w, tab, ls, send, recv, near_send, near_recv, bulk_send, bulk_recv, local,
):
    r, v = lax.axis_index("rows"), lax.axis_index("vocab")
    z, x = lax.div(r, 2), lax.rem(r, 2) * 2 + lax.div(v, 8)
    y, c = lax.rem(lax.div(v, 2), NY), lax.rem(v, 2)
    other = 1 - c
    sizes = {"x": NX, "y": NY, "z": NZ}
    here = {"x": x, "y": y, "z": z}

    def away(dx=0, dy=0, dz=0, dc=0):
        return place(
            shifted(x, dx, NX), shifted(y, dy, NY), shifted(z, dz, NZ), c if dc == 0 else other
        )

    x_lo = lax.rem(x, 2)
    q2_slot = jnp.where(lax.rem(z, 2) == 0, 8, 20) + lax.div(z, 2)
    own_slots = (z, q2_slot, 12 + z)

    fills = []

    def fill(source, target):
        copy = pltpu.make_async_copy(source, target, local.at[len(fills)])
        copy.start()
        fills.append(copy)
        return copy

    quarter = [hid.at[:, pl.ds(128 * q, 128)] for q in range(4)]
    for q, slot in zip((1, 2, 3), own_slots):
        fill(quarter[q], g.at[c, x, y, slot])
    fill(quarter[0], ha.at[c, z, y, x])
    fill(st_in, raw)
    tab_fill = fill(tab_in, tab)
    w_fill = fill(w_in, w)

    barrier = pltpu.get_barrier_semaphore()
    friends = [away(i, j, 0, k) for i, j, k in PLANE_CORES] + [away(dz=s) for s in COLUMN]
    for friend in friends:
        pl.semaphore_signal(barrier, inc=1, device_id=friend, device_id_type=MESH)
    pl.semaphore_wait(barrier, len(friends))
    for copy in fills[:5]:
        copy.wait()
    st[x_lo, y, c] = jnp.broadcast_to(jnp.concatenate([raw[...]] * 4, axis=1), (8, 128))

    count, near_count = itertools.count(), itertools.count()
    sent = []

    def remote(source, target, device, send_sem, recv_sem):
        copy = pltpu.make_async_remote_copy(
            src_ref=source, dst_ref=target, send_sem=send_sem, recv_sem=recv_sem,
            device_id=device, device_id_type=MESH,
        )
        copy.start()
        return copy

    def arrived(target, sem):
        pltpu.make_async_copy(target, target, sem).wait()

    clock = [0.0]
    queue = []
    order = itertools.count()
    links = {}

    def post(time, action, rank=0):
        heapq.heappush(queue, (time, rank, next(order), action))

    def through(link, nbytes, rate, latency):
        links[link] = max(clock[0], links.get(link, 0.0)) + nbytes / rate
        return links[link] + latency

    for s in COLUMN:
        for slot in own_slots:
            block = g.at[c, x, y, slot]
            remote(block, block, away(dz=s), bulk_send.at[0], bulk_recv.at[0])
    own_tile = st.at[x_lo, y, c]
    for i, j in PLANE:
        block = ha.at[c, z, y, x]
        remote(block, block, away(i, j), bulk_send.at[1], bulk_recv.at[1])
    x_other = 1 - 2 * x_lo
    for lo in (1, 0):
        for j in range(NY):
            for k in range(2):
                if (lo, j, k) != (0, 0, 0):
                    device = place(
                        x + x_other if lo else x, shifted(y, j, NY), z, c if k == 0 else other
                    )
                    remote(own_tile, own_tile, device, bulk_send.at[2], bulk_recv.at[2])

    done = set()
    near_at = {}
    tasks = []

    def near_landed(unit):
        done.add(unit)
        for task in list(tasks):
            needs, action = task
            if all(n in done for n in needs):
                tasks.remove(task)
                post(clock[0], action, 1)

    def hand_over(unit, piece, nbytes):
        index = next(near_count)
        source = piece(c)
        sent.append(remote(source, source, away(dc=1), near_send.at[index], near_recv.at[index]))
        near_at[unit] = (piece(other), index)
        post(through("near", nbytes, NEAR, NEAR_HOP), lambda: near_landed(unit))

    def take(units):
        for unit in units:
            if unit in near_at:
                target, index = near_at.pop(unit)
                arrived(target, near_recv.at[index])

    def spread(axis, way, d, h, pieces, piece, nbytes, seen):
        size = sizes[axis]
        half = size // 2
        index = next(count)
        source = piece(shifted(here[axis], -way * (d - 1), size), h)
        device = away(**{"d" + axis: way})
        sent.append(remote(source, source, device, send.at[index], recv.at[index]))

        def land():
            origin = shifted(here[axis], -way * d, size)
            arrived(piece(origin, h), recv.at[index])
            final = h < pieces // 2 if way > 0 else h >= pieces // 2
            if d + 1 < half or (d + 1 == half and final):
                spread(axis, way, d + 1, h, pieces, piece, nbytes, seen)
            seen(-way * d if d < half else half, origin, h)

        post(through((axis, way), nbytes, LINK, FIRST_HOP), land)

    def around(axis, pieces, piece, nbytes, seen):
        for i in range(pieces):
            spread(axis, 1, 1, i, pieces, piece, nbytes, seen)
            spread(axis, -1, 1, pieces - 1 - i, pieces, piece, nbytes, seen)

    block_bytes = 32 * 128 * 2
    unit_bytes = 6 * block_bytes

    def unit_piece(xx, yy, k):
        return lambda core: g.at[core, xx, yy, pl.ds(6 * k, 6)]

    def column_ready():
        arrived(g.at[c, x, y, pl.ds(0, 21)], bulk_recv.at[0])

        def colour(first, last, ks):
            def at(p_first, p_last, k):
                where = {first: p_first, last: p_last}
                return unit_piece(where["x"], where["y"], k)

            def onward(rel_first, p_first, h):
                k = ks[h]

                def seen(rel_last, p_last, _):
                    rel = {first: rel_first, last: rel_last}
                    hand_over((rel["x"], rel["y"], k), at(p_first, p_last, k), unit_bytes)

                for way in (1, -1):
                    spread(
                        last, way, 1, h, 2, lambda p, hh: at(p_first, p, ks[hh])(c), unit_bytes, seen,
                    )

            def seen_first(rel_first, p_first, h):
                onward(rel_first, p_first, h)
                rel = {first: rel_first, last: 0}
                hand_over((rel["x"], rel["y"], ks[h]), at(p_first, here[last], ks[h]), unit_bytes)

            return (
                lambda: around(
                    first, 2, lambda p, h: at(p, here[last], ks[h])(c), unit_bytes, seen_first
                ),
                lambda: [onward(0, here[first], h) for h in range(2)],
            )

        b_first, b_last = colour("y", "x", (0, 1))
        c_first, c_last = colour("x", "y", (2, 3))
        b_first()
        c_first()
        b_last()
        c_last()
        for k in range(4):
            hand_over((0, 0, k), unit_piece(x, y, k), unit_bytes)

    def plane_ready():
        arrived(g.at[c, x, y, pl.ds(0, 15)], bulk_recv.at[1])
        piece = lambda core, p, h: ha.at[core, p, pl.ds(2 * h, 2)]

        def seen(rel, p, h):
            hand_over(("a", rel, h), lambda core: piece(core, p, h), 8 * block_bytes)

        around("z", 2, lambda p, h: piece(c, p, h), 8 * block_bytes, seen)
        hand_over(("a", 0, 0), lambda core: ha.at[core, z], 16 * block_bytes)

    def weights(offsets):
        return jnp.concatenate(
            [w[:, pl.ds(pl.multiple_of(o, 128), 128)] for o in offsets], axis=1
        )

    def stack(parts):
        return jnp.concatenate(parts, axis=0)

    def a_task(zz):
        rhs = jnp.concatenate(
            [
                stack(
                    [
                        ha[core, zz, yy, 2 * hi + lo]
                        for lo in range(2) for yy in range(NY) for core in range(2)
                    ]
                )
                for hi in range(2)
            ],
            axis=1,
        )
        lhs = weights([(2 * zz + hi) * 512 for hi in range(2)])
        acc_out[...] += lax.dot_general(lhs, rhs, NT, preferred_element_type=jnp.float32)

    def column_of(slot, hi):
        if slot < 8:
            return (2 * slot + hi) * 512 + 128
        if slot < 12:
            return (4 * (slot - 8) + hi) * 512 + 256
        if slot < 20:
            return (2 * (slot - 12) + hi) * 512 + 384
        return (4 * (slot - 20) + 2 + hi) * 512 + 256

    def b_task(xx, k):
        hi, lo = lax.div(xx, 2), lax.rem(xx, 2)
        slots = range(6 * k, 6 * k + 6)
        rhs = jnp.concatenate(
            [stack([g[core, xx, yy, s] for yy in range(NY) for core in range(2)]) for s in slots],
            axis=1,
        )
        lanes = pl.ds(pl.multiple_of(lo * 256, 128), 256)
        acc_out[:, lanes] += lax.dot_general(
            weights([column_of(s, hi) for s in slots]), rhs, NT, preferred_element_type=jnp.float32
        )

    def c_task(hi, pair, k):
        slots = range(6 * k, 6 * k + 6)
        rhs = jnp.concatenate(
            [
                stack(
                    [
                        g[core, 2 * hi + lo, 2 * pair + yy, s]
                        for lo in range(2) for yy in range(2) for core in range(2)
                    ]
                )
                for s in slots
            ],
            axis=1,
        )
        out = lax.dot_general(
            weights([column_of(s, hi) for s in slots]), rhs, NT, preferred_element_type=jnp.float32
        )
        for lo in range(2):
            lanes = pl.ds(pl.multiple_of(lo * 256 + pair * 128, 128), 128)
            acc_out[:, lanes] += out[:, lo * 128 : (lo + 1) * 128]

    def add_task(needs, cost, work):
        def action():
            take(needs)
            work()
            clock[0] += cost

        tasks.append((needs, action))

    for rel in (0, 1, -1, 2, -2, 3, -3, 4):
        needs = [("a", rel, h) for h in range(2)] if rel else [("a", 0, 0)]
        add_task(
            ["start"] + needs, A_TASK, lambda rel=rel: a_task(shifted(z, rel, NZ))
        )
    for rel in (0, 1, -1, 2):
        for k in (0, 1):
            add_task(
                ["start"] + [(rel, dy, k) for dy in (0, 1, -1, 2)], G_TASK,
                lambda rel=rel, k=k: b_task(shifted(x, rel, NX), k),
            )
    close, far = (0, 1, -1), (1, -1, 2)
    for dxs in (close, far):
        for dys in (close, far):
            for k in (2, 3):
                add_task(
                    ["start"] + [(dx, dy, k) for dx in dxs for dy in dys], G_TASK,
                    lambda dxs=dxs, dys=dys, k=k: c_task(
                        lax.div(x, 2) if dxs is close else 1 - lax.div(x, 2),
                        lax.div(y, 2) if dys is close else 1 - lax.div(y, 2),
                        k,
                    ),
                )

    def begin():
        arrived(ls.at[pl.ds(1, 30)], bulk_recv.at[2])
        tab_fill.wait()
        group = lax.div(lax.broadcasted_iota(jnp.int32, (1, 128), 1), 32)
        parts = []
        for lo in range(2):
            for pair in range(2):
                picked = st[lo, 2 * pair + 1, 1, 0:1]
                for k in range(3):
                    picked = jnp.where(group == k, st[lo, 2 * pair + k // 2, k % 2, 0:1], picked)
                parts.append(picked)
        row_states = jnp.concatenate(parts, axis=1)
        marks = lax.broadcasted_iota(jnp.int32, (tab.shape[1], row_states.shape[1]), 0)
        onehot = jnp.where(marks == row_states, 1.0, 0.0).astype(jnp.bfloat16)
        allowed = jnp.dot(
            tab[...].astype(jnp.float32).astype(jnp.bfloat16), onehot, preferred_element_type=jnp.float32
        )
        acc_out[...] = jnp.where(allowed > 0.5, 0.0, LOWEST)
        w_fill.wait()
        clock[0] += 1.0
        near_landed("start")

    post(6.0, plane_ready)
    post(7.0, column_ready)
    post(6.5, begin)
    while queue:
        time, _, _, action = heapq.heappop(queue)
        clock[0] = max(clock[0], time)
        action()

    own = ls.at[0]
    for k in range(4):
        tile = acc_out[:, pl.ds(128 * k, 128)]
        peak = jnp.max(tile, axis=0, keepdims=True)
        own[k : k + 1] = peak + jnp.log(jnp.sum(jnp.exp(tile - peak), axis=0, keepdims=True))

    def combine(first, number):
        values = ls[first : first + number]
        peak = jnp.max(values, axis=0)
        return peak + jnp.log(jnp.sum(jnp.exp(values - peak[None]), axis=0))

    for n, (i, j, k) in enumerate(PLANE_CORES):
        remote(own, ls.at[1 + n], away(i, j, 0, k), bulk_send.at[3], bulk_recv.at[3])
    arrived(ls.at[pl.ds(1, 31)], bulk_recv.at[3])
    mine = ls.at[32]
    mine[...] = combine(0, 32)
    for n, s in enumerate(COLUMN):
        remote(mine, ls.at[33 + n], away(dz=s), bulk_send.at[4], bulk_recv.at[4])
    arrived(ls.at[pl.ds(33, 7)], bulk_recv.at[4])
    norm = combine(32, 8)
    for k in range(4):
        norm_out[0:1, pl.ds(128 * k, 128)] = norm[k : k + 1]

    for copy in sent:
        copy.wait_send()
    arrived(g.at[c, x, y, pl.ds(0, 21)], bulk_send.at[0])
    arrived(g.at[c, x, y, pl.ds(0, 15)], bulk_send.at[1])
    arrived(ls.at[pl.ds(1, 30)], bulk_send.at[2])
    arrived(ls.at[pl.ds(1, 31)], bulk_send.at[3])
    arrived(ls.at[pl.ds(33, 7)], bulk_send.at[4])


def local(hidden_rows, row_states, head_weight, grammar_table):
    depth, columns = head_weight.shape
    states = grammar_table.shape[0]
    rows = 512
    operands = (hidden_rows, row_states[None, :], head_weight.T, grammar_table.T)
    anywhere = pl.BlockSpec(memory_space=pl.ANY)
    inside = pl.BlockSpec(memory_space=pltpu.VMEM)
    masked, norm = pl.pallas_call(
        kernel,
        out_shape=(
            jax.ShapeDtypeStruct((columns, rows), jnp.float32),
            jax.ShapeDtypeStruct((1, rows), jnp.float32),
        ),
        in_specs=[anywhere] * 4,
        out_specs=(inside, inside),
        scratch_shapes=[
            pltpu.VMEM((2, NZ, NY, NX, 32, 128), jnp.bfloat16),
            pltpu.VMEM((2, NX, NY, 24, 32, 128), jnp.bfloat16),
            pltpu.VMEM((2, NY, 2, 8, 128), jnp.int32),
            pltpu.VMEM((1, 32), jnp.int32),
            pltpu.VMEM((columns, depth), jnp.bfloat16),
            pltpu.VMEM((columns, states), jnp.int32),
            pltpu.VMEM((40, 4, 128), jnp.float32),
            pltpu.SemaphoreType.DMA((92,)),
            pltpu.SemaphoreType.DMA((92,)),
            pltpu.SemaphoreType.DMA((96,)),
            pltpu.SemaphoreType.DMA((96,)),
            pltpu.SemaphoreType.DMA((5,)),
            pltpu.SemaphoreType.DMA((5,)),
            pltpu.SemaphoreType.DMA((8,)),
        ],
        compiler_params=pltpu.CompilerParams(
            collective_id=0, has_side_effects=True, vmem_limit_bytes=40 << 20
        ),
    )(*(pltpu.with_memory_space_constraint(a, pltpu.HBM) for a in operands))
    log_probs = jnp.where(masked > 0.5 * LOWEST, masked - norm, 0.0)
    return (log_probs.T, norm[0])


def solution(mesh):
    placed = (
        P("vocab", "rows"),
        P("vocab"),
        P(None, ("rows", "vocab")),
        P(None, ("rows", "vocab")),
    )
    return jax.shard_map(
        local,
        mesh=mesh,
        in_specs=placed,
        out_specs=(P(None, ("rows", "vocab")), P()),
        check_vma=False,
    )
```
